32 devices in a mesh: dp: 16 (over z, x, core), mp: 2 (over y).
Axes of the slice: x: 2, y: 2, z: 4, core: 2. Of those that a mesh axis runs over, the one named last changes fastest.
Arguments:
- hidden_in: bfloat16 [16, 1024, 512], P('dp'), may hold values from -6 to 6
- memory: bfloat16 [16, 1024, 512], P('dp'), may hold values from -6 to 6
- tgt_lengths: int32 [16, 8], P('dp'), may hold values from 1 to 256, 1024 in all within a row
- src_lengths: int32 [16, 8], P('dp'), may hold values from 1 to 256, 1024 in all within a row
- timesteps: int32 [16, 8], P('dp'), may hold values from 1 to 50
- out_grad: bfloat16 [16, 1024, 512], P('dp'), may hold values from -6 to 6
- norm_gain: float32 [3, 512], replicated, may hold values from 0.5 to 1.5
- norm_bias: float32 [3, 512], replicated, may hold values from -3 to 3
- self_qkv: bfloat16 [512, 3, 512], P(None, None, 'mp'), may hold values from -0.375 to 0.375
- self_bias: float32 [2, 512], P(None, 'mp'), may hold values from -3 to 3
- self_out: bfloat16 [512, 512], P('mp'), may hold values from -0.5 to 0.5
- cross_q: bfloat16 [512, 512], P(None, 'mp'), may hold values from -0.375 to 0.375
- cross_kv: bfloat16 [512, 2, 512], P(None, None, 'mp'), may hold values from -0.375 to 0.375
- cross_bias: float32 [2, 512], P(None, 'mp'), may hold values from -3 to 3
- cross_out: bfloat16 [512, 512], P('mp'), may hold values from -0.5 to 0.5
- ffn_in: bfloat16 [512, 2048], P(None, 'mp'), may hold values from -0.25 to 0.25
- ffn_in_bias: float32 [2048], P('mp'), may hold values from -3 to 3
- ffn_out: bfloat16 [2048, 512], P('mp'), may hold values from -0.125 to 0.125
- out_bias: float32 [3, 512], replicated, may hold values from -3 to 3
Outputs:
- block_out: bfloat16 [16, 1024, 512], P('dp')
- input_grad: float32 [16, 1024, 512], P('dp')
- memory_grad: float32 [16, 1024, 512], P('dp')
- norm_gain_grad: float32 [3, 512], replicated
- norm_bias_grad: float32 [3, 512], replicated
- self_qkv_grad: float32 [512, 3, 512], P(None, None, 'mp')
- self_bias_grad: float32 [2, 512], P(None, 'mp')
- self_out_grad: float32 [512, 512], P('mp')
- cross_q_grad: float32 [512, 512], P(None, 'mp')
- cross_kv_grad: float32 [512, 2, 512], P(None, None, 'mp')
- cross_bias_grad: float32 [2, 512], P(None, 'mp')
- cross_out_grad: float32 [512, 512], P('mp')
- ffn_in_grad: float32 [512, 2048], P(None, 'mp')
- ffn_in_bias_grad: float32 [2048], P('mp')
- ffn_out_grad: float32 [2048, 512], P('mp')
- out_bias_grad: float32 [3, 512], replicated
The draws below stay inside these ranges and needn't reach their ends.
Inputs may be any that keep to these rules, and one draw needn't show every extreme that they name: `tgt_lengths`: each row's target slots hold 8 sentences laid end to end from slot 0, summing to 1024; the last one is padding; the longest in each row has 256 slots. `src_lengths`: each row's source slots hold 8 sentences summing to 1024; source sentence k belongs to target sentence k; the longest has 256 slots.
All inputs are finite; a program needn't handle non-finite values.
Results may differ from the reference program's by a relative error of at most 0.038.
Values may be sent and summed in bfloat16 or wider, within the bound.
No kernel may reach another device: no remote copies, remote signals or barrier semaphores. Data moves between devices by JAX's collectives and lax.ppermute only.
A program may use at most 192 MiB of HBM per device.

```python
import math
import jax
import jax.numpy as jnp
import numpy as np
from jax import lax

D = 512
HEADS = 8
HEAD_DIM = 64
FF = 2048
SLOTS = 1024
SRC = 1024
NSEG = 8
LMAX = 256
LMAX_SRC = 256
TSTEPS = 50
ROWS = 16
N_MP = 2


def with_ends(values, own_key, smallest, high):
    index_at = [jax.random.randint(jax.random.fold_in(own_key, axis), (), 0, length) for axis, length in enumerate(values.shape)]
    widest = values.shape.index(max(values.shape))
    next_to = index_at[:widest] + [(index_at[widest] + 1) % values.shape[widest]] + index_at[widest + 1:]
    return values.at[tuple(index_at)].set(smallest).at[tuple(next_to)].set(high)


def steps_of(rng, dims, cuts, low, largest):
    level, own = 1.0, jax.random.fold_in(rng, 6)
    for axis_at, blocks in cuts:
        heights = jnp.exp(jax.random.uniform(jax.random.fold_in(own, axis_at), (blocks,), jnp.float32, low / len(cuts), largest / len(cuts)))
        level = level * jnp.repeat(heights, dims[axis_at] // blocks).reshape([-1 if axis == axis_at else 1 for axis in range(len(dims))])
    return level


def length_profile(amount, total, bound, slope):
    loads = [(1 << 20) // math.isqrt(rank ** slope) + 1 for rank in range(2, amount + 1)]
    surplus, counts = total - bound - (amount - 1), [1] * (amount - 1)
    while surplus > 0:
        movable = [i for i in range(amount - 1) if counts[i] < bound]
        pool, left = sum([loads[i] for i in movable]), surplus
        for i in movable:
            extra = min(bound - counts[i], max(1, left * loads[i] // pool), surplus)
            counts[i] = counts[i] + extra
            surplus = surplus - extra
    return np.array([bound] + counts)


def uneven(rng, count, total, bound, slope):
    if count == 2:
        one = jax.random.randint(rng, (), max(1, total - bound), min(bound, total - 1) + 1)
        return jnp.stack([one, total - one])
    sizes = jnp.asarray(length_profile(count, total, bound, slope), jnp.int32)
    pairs = (count - 1) // 2
    donor, taker = sizes[1:1 + 2 * pairs:2], sizes[2:2 + 2 * pairs:2]
    margin = jnp.minimum(donor - 1, bound - taker)
    moved = jax.random.randint(jax.random.fold_in(rng, 1), (pairs,), 0, 1 << 20) % (margin + 1)
    sizes = sizes.at[1:1 + 2 * pairs:2].set(donor - moved).at[2:2 + 2 * pairs:2].set(taker + moved)
    return sizes[jax.random.permutation(jax.random.fold_in(rng, 2), count)]


def scatter_about(key, shape, spread, reach, split=(), kind=jnp.bfloat16):
    drawn = spread * jax.random.normal(key, shape, jnp.float32)
    if split:
        drawn = drawn * steps_of(key, shape, split, -0.22, 0.18)
    return jnp.clip(drawn, -reach, reach).astype(kind)


def setup_inputs(seed: int = 0) -> dict:
    keys = jax.random.split(jax.random.key(seed), 20)
    return {
        "hidden_in": scatter_about(keys[0], (ROWS, SLOTS, D), 1.0, 6.0, ((0, 16),)),
        "memory": scatter_about(keys[1], (ROWS, SRC, D), 1.0, 6.0, ((0, 16),)),
        "tgt_lengths": jax.vmap(lambda own: uneven(own, NSEG, SLOTS, LMAX, 2))(jax.random.split(keys[2], ROWS)).reshape((ROWS, NSEG)).astype(jnp.int32),
        "src_lengths": jax.vmap(lambda own: uneven(own, NSEG, SRC, LMAX_SRC, 2))(jax.random.split(keys[3], ROWS)).reshape((ROWS, NSEG)).astype(jnp.int32),
        "timesteps": with_ends(jax.random.randint(keys[4], (ROWS, NSEG), 1, TSTEPS + 1), jax.random.fold_in(keys[4], 1), 1, TSTEPS).astype(jnp.int32),
        "out_grad": scatter_about(keys[5], (ROWS, SLOTS, D), 1.0, 6.0, ((0, 16),)),
        "norm_gain": jnp.clip(1.0 + 0.1 * jax.random.normal(keys[6], (3, D), jnp.float32), 0.5, 1.5),
        "norm_bias": scatter_about(keys[7], (3, D), 0.5, 3.0, (), jnp.float32),
        "self_qkv": scatter_about(keys[8], (D, 3, D), (D // 2) ** -0.5, 0.375, ((2, 2),)),
        "self_bias": scatter_about(keys[9], (2, D), 0.5, 3.0, ((1, 2),), jnp.float32),
        "self_out": scatter_about(keys[10], (D, D), (D // 4) ** -0.5, 0.5, ((0, 2),)),
        "cross_q": scatter_about(keys[11], (D, D), (D // 2) ** -0.5, 0.375, ((1, 2),)),
        "cross_kv": scatter_about(keys[12], (D, 2, D), (D // 2) ** -0.5, 0.375, ((2, 2),)),
        "cross_bias": scatter_about(keys[13], (2, D), 0.5, 3.0, ((1, 2),), jnp.float32),
        "cross_out": scatter_about(keys[14], (D, D), (D // 4) ** -0.5, 0.5, ((0, 2),)),
        "ffn_in": scatter_about(keys[15], (D, FF), D ** -0.5, 0.25, ((1, 2),)),
        "ffn_in_bias": scatter_about(keys[16], (FF,), 0.5, 3.0, ((0, 2),), jnp.float32),
        "ffn_out": scatter_about(keys[17], (FF, D), FF ** -0.5, 0.125, ((0, 2),)),
        "out_bias": scatter_about(keys[18], (3, D), 0.5, 3.0, (), jnp.float32),
    }


@jax.custom_vjp
def low(v):
    return lax.optimization_barrier(v.astype(jnp.bfloat16)).astype(jnp.float32)

@jax.custom_vjp
def low_back(v):
    return v

def low_keep(v):
    return (low(v), None)

def low_pass(kept, grad):
    return (grad,)

def back_keep(v):
    return (v, None)

def back_low(kept, grad):
    return (low(grad),)
low.defvjp(low_keep, low_pass)
low_back.defvjp(back_keep, back_low)

def matmul(left, right):
    return jnp.dot(left, right, precision=lax.Precision.HIGHEST)

def rounded_both(value):
    return low(low_back(value))

def layer_norm(value, gain, shift):
    row_mean = lax.optimization_barrier(jnp.mean(value, axis=-1, keepdims=True))
    center = value - row_mean
    variance = lax.optimization_barrier(jnp.mean(center * center, axis=-1, keepdims=True))
    return center * lax.rsqrt(variance + 1e-05) * gain + shift

def segments_of(lengths, count):
    seg_ends = jnp.cumsum(lengths).astype(jnp.int32)
    places = jnp.arange(count, dtype=jnp.int32)
    return lax.optimization_barrier(jnp.sum((places[:, None] >= seg_ends[None, :]).astype(jnp.int32), axis=1)).astype(jnp.int32)

def time_embedding(steps, model_width):
    half_width = model_width // 2
    frequency = jnp.exp(-math.log(10000.0) * jnp.arange(half_width, dtype=jnp.float32) / half_width)
    angles = steps[:, None] * frequency[None, :]
    return jnp.concatenate([jnp.sin(angles), jnp.cos(angles)], axis=1)

def attend(queries, key_rows, value_rows, allowed):
    score_scale = HEAD_DIM ** (-0.5)
    raw_scores = jnp.einsum('she,the->hst', queries, key_rows, precision=lax.Precision.HIGHEST)
    scores = low_back(raw_scores * score_scale)
    scores = jnp.where(allowed[None], scores, -1000000000.0)
    weights = jax.nn.softmax(scores, axis=-1)
    return jnp.einsum('hst,the->she', low(weights), value_rows, precision=lax.Precision.HIGHEST)

def split_heads(values):
    return values.reshape(values.shape[0], HEADS, HEAD_DIM)

def project_out(heads_in, weight, bias):
    count = heads_in.shape[0]
    group_width = heads_in.shape[1] // N_MP
    pieces = heads_in.reshape(count, N_MP, group_width)
    weight_pieces = weight.reshape(N_MP, group_width, weight.shape[1])
    partials = jnp.einsum('sgc,gcd->gsd', pieces, weight_pieces, precision=lax.Precision.HIGHEST)
    return low_back(lax.optimization_barrier(jnp.sum(low(partials), axis=0)) + bias)

def row_forward(hidden, memory_row, tgt_segment, src_segment, real_mask, time_rows, params):
    norm_gain, norm_bias, self_qkv, self_bias, self_out, cross_q, cross_kv, cross_bias, cross_out, ffn_in, ffn_in_bias, ffn_out, out_bias = params
    slot_count = hidden.shape[0]
    resid_zero = hidden + time_rows
    normed_one = low(layer_norm(resid_zero, norm_gain[0], norm_bias[0]))
    projected = jnp.einsum('sd,dke->ske', normed_one, self_qkv, precision=lax.Precision.HIGHEST)
    queries = rounded_both(projected[:, 0] + self_bias[0])
    key_rows = rounded_both(projected[:, 1])
    value_rows = rounded_both(projected[:, 2] + self_bias[1])
    allowed = tgt_segment[:, None] == tgt_segment[None, :]
    mixed = attend(split_heads(queries), split_heads(key_rows), split_heads(value_rows), allowed)
    self_heads = rounded_both(mixed.reshape(slot_count, HEADS * HEAD_DIM))
    resid_one = resid_zero + real_mask[:, None] * project_out(self_heads, self_out, out_bias[0])
    normed_two = low(layer_norm(resid_one, norm_gain[1], norm_bias[1]))
    cross_queries = rounded_both(matmul(normed_two, cross_q) + cross_bias[0])
    memory_proj = jnp.einsum('sd,dke->ske', memory_row, cross_kv, precision=lax.Precision.HIGHEST)
    cross_keys = rounded_both(memory_proj[:, 0])
    cross_values = rounded_both(memory_proj[:, 1] + cross_bias[1])
    allowed_cross = tgt_segment[:, None] == src_segment[None, :]
    mixed_cross = attend(split_heads(cross_queries), split_heads(cross_keys), split_heads(cross_values), allowed_cross)
    cross_heads = rounded_both(mixed_cross.reshape(slot_count, HEADS * HEAD_DIM))
    resid_two = resid_one + real_mask[:, None] * project_out(cross_heads, cross_out, out_bias[1])
    normed_three = low(layer_norm(resid_two, norm_gain[2], norm_bias[2]))
    inner_pre = low_back(matmul(normed_three, ffn_in) + ffn_in_bias)
    activation = low(jax.nn.gelu(inner_pre, approximate=False))
    return resid_two + real_mask[:, None] * project_out(activation, ffn_out, out_bias[2])

def reference(hidden_in, memory, tgt_lengths, src_lengths, timesteps, out_grad, norm_gain, norm_bias, self_qkv, self_bias, self_out, cross_q, cross_kv, cross_bias, cross_out, ffn_in, ffn_in_bias, ffn_out, out_bias):
    params = tuple((weight.astype(jnp.float32) for weight in (norm_gain, norm_bias, self_qkv, self_bias, self_out, cross_q, cross_kv, cross_bias, cross_out, ffn_in, ffn_in_bias, ffn_out, out_bias)))

    def one_row(totals, row_items):
        hidden, memory_row, tgt_row, src_row, step_row, cotangent = row_items
        tgt_segment = segments_of(tgt_row, SLOTS)
        src_segment = segments_of(src_row, SRC)
        real_mask = (tgt_segment < NSEG - 1).astype(jnp.float32)
        chosen = tgt_segment[:, None] == jnp.arange(NSEG, dtype=jnp.int32)[None, :]
        steps = lax.optimization_barrier(jnp.sum(jnp.where(chosen, step_row[None, :], 0), axis=1)).astype(jnp.float32)
        time_rows = time_embedding(steps, D)

        def forward(hidden_value, memory_value, weights):
            return row_forward(hidden_value, memory_value, tgt_segment, src_segment, real_mask, time_rows, weights)
        output, pullback = jax.vjp(forward, hidden.astype(jnp.float32), memory_row.astype(jnp.float32), params)
        hidden_grad, memory_grad, weight_grads = pullback(cotangent.astype(jnp.float32))
        totals = jax.tree.map(jnp.add, totals, weight_grads)
        return (totals, (output.astype(jnp.bfloat16), hidden_grad, memory_grad))
    zero_totals = jax.tree.map(jnp.zeros_like, params)
    totals, (block_out, input_grad, memory_grad) = lax.scan(one_row, zero_totals, (hidden_in, memory, tgt_lengths, src_lengths, timesteps, out_grad))
    return (block_out, input_grad, memory_grad, totals[0], totals[1], totals[2], totals[3], totals[4], totals[5], totals[6], totals[7], totals[8], totals[9], totals[10], totals[11], totals[12])
```

```python
from functools import partial
import math

import jax
import jax.numpy as jnp
from jax import lax
from jax.experimental import pallas as pl
from jax.experimental.pallas import tpu as pltpu
from jax.sharding import PartitionSpec as P

HEAD_DIM = 64
LONGEST = 256


NEG = -1000000000.0
F32, BF16 = jnp.float32, jnp.bfloat16
CHUNK = 128


def segments_of(lengths, count):
    seg_ends = jnp.cumsum(lengths, axis=-1)
    places = jnp.arange(count, dtype=jnp.int32)
    return jnp.sum((places[None, :, None] >= seg_ends[:, None, :]).astype(jnp.int32), axis=2)


def time_embedding(steps, model_width):
    half_width = model_width // 2
    frequency = jnp.exp(-math.log(10000.0) * jnp.arange(half_width, dtype=jnp.float32) / half_width)
    angles = steps[:, None] * frequency[None, :]
    return jnp.concatenate([jnp.sin(angles), jnp.cos(angles)], axis=1)


def dot(left, right, contract=(1, 0), precision=None):
    return lax.dot_general(
        left,
        right,
        (((contract[0],), (contract[1],)), ((), ())),
        preferred_element_type=F32,
        precision=precision,
    )


def rows_at(step, size=CHUNK):
    return pl.ds(pl.multiple_of(step * size, size), size)


def part_lanes(part):
    return pl.ds(pl.multiple_of(part * 128, 128), 128)


def low_lanes(rows):
    return lax.broadcasted_iota(jnp.int32, (rows, 128), 1) < HEAD_DIM


def head_split(value, low):
    zero = jnp.zeros_like(value)
    return jnp.where(low, value, zero), jnp.where(low, zero, value)


def norm_rows(value):
    center = value - jnp.mean(value, axis=-1, keepdims=True)
    scale = lax.rsqrt(jnp.mean(center * center, axis=-1, keepdims=True) + 1e-05)
    return center * scale, scale


def norm_back(grad, gain, xhat, scale):
    scaled = grad * gain
    return scale * (
        scaled
        - jnp.mean(scaled, axis=-1, keepdims=True)
        - xhat * jnp.mean(scaled * xhat, axis=-1, keepdims=True)
    )


def sum_rows(value):
    return jnp.sum(value, axis=0, keepdims=True)


def unpack_weights(packs, outs, out_ref):
    width = out_ref.shape[1]
    for part, pack in enumerate(packs):
        lanes = slice(part * 128, part * 128 + 128)
        for kind, ref in enumerate(outs):
            ref[:, lanes] = pack[kind * width : (kind + 1) * width]
        for block in range(width // 128):
            at = len(outs) * width + block * 128
            out_ref[lanes, block * 128 : block * 128 + 128] = pack[at : at + 128]


def store_grads(grads, out_grad, kept, given):
    width = out_grad.shape[1]
    rows = (len(grads) + 1) * width
    for part in range(4):
        ref, base = (kept, given)[part % 2], (part // 2) * rows
        lanes = slice(part * 128, part * 128 + 128)
        for kind, ref_in in enumerate(grads):
            at = base + kind * width
            ref[at : at + width] = ref_in[:, lanes]
        for block in range(width // 128):
            at = base + len(grads) * width + block * 128
            ref[at : at + 128] = out_grad[lanes, block * 128 : block * 128 + 128]


def attend_rows(q_ref, k_ref, v_ref, q_seg, k_seg, heads_ref, lse_ref, lse_rows, block):
    slots, keys = q_ref.shape[0], k_ref.shape[0]
    lane = lax.broadcasted_iota(jnp.int32, (block, 128), 1)
    lse_rows[...] = jnp.zeros_like(lse_rows)

    def one_part(part, carry):
        lanes = part_lanes(part)
        key = k_ref[:, lanes]
        values = head_split(v_ref[:, lanes], low_lanes(keys))

        def one_block(step, carry):
            rows = rows_at(step, block)
            allowed = q_seg[rows, :] == k_seg[...]
            queries = head_split(q_ref[rows, lanes], low_lanes(block))
            mixed = jnp.zeros((block, 128), F32)
            totals = lse_rows[rows, :]
            for head in range(2):
                scores = jnp.where(allowed, dot(queries[head], key, (1, 1)), NEG)
                highest = jnp.max(scores, axis=-1, keepdims=True)
                raised = jnp.exp(scores - highest)
                total = jnp.sum(raised, axis=-1, keepdims=True)
                mixed = mixed + dot(raised.astype(BF16), values[head]) / total
                totals = jnp.where(lane == 2 * part + head, highest + jnp.log(total), totals)
            heads_ref[rows, lanes] = mixed.astype(BF16)
            lse_rows[rows, :] = totals
            return carry

        return lax.fori_loop(0, slots // block, one_block, carry)

    lax.fori_loop(0, 4, one_part, 0)
    lse_ref[...] = jnp.transpose(lse_rows[...])[: lse_ref.shape[0]]


def attend_back(
    q_ref, k_ref, v_ref, u_ref, heads_ref, lse_ref, q_seg, k_seg, dq_ref, dk_ref, dv_ref, acc, delta, block
):
    slots, keys = q_ref.shape[0], k_ref.shape[0]
    width = q_ref.shape[1]
    heads = width // HEAD_DIM
    of_head = lax.broadcasted_iota(jnp.int32, (heads, width), 1) // HEAD_DIM
    pick = (of_head == lax.broadcasted_iota(jnp.int32, (heads, width), 0)).astype(F32)
    product = u_ref[...].astype(F32) * heads_ref[...].astype(F32)
    delta[...] = dot(pick, product, (1, 1), lax.Precision.HIGHEST)

    def one_part(part, carry):
        lanes = part_lanes(part)
        queries = head_split(q_ref[:, lanes], low_lanes(slots))
        upper = head_split(u_ref[:, lanes], low_lanes(slots))
        acc[...] = jnp.zeros_like(acc)

        def one_block(step, carry):
            rows = rows_at(step, block)
            allowed = k_seg[rows, :] == q_seg[...]
            key, value = k_ref[rows, lanes], v_ref[rows, lanes]
            split_keys = head_split(key, low_lanes(block))
            dk = jnp.zeros((block, 128), F32)
            dv = jnp.zeros((block, 128), F32)
            total = acc[...]
            for head in range(2):
                at = pl.ds(2 * part + head, 1)
                scores = jnp.where(allowed, dot(key, queries[head], (1, 1)), NEG)
                weights = jnp.exp(scores - lse_ref[at, :])
                dv = dv + dot(weights.astype(BF16), upper[head])
                change = dot(value, upper[head], (1, 1)) - delta[at, :]
                change = (weights * change).astype(BF16)
                dk = dk + dot(change, queries[head])
                total = total + dot(change, split_keys[head], (0, 0))
            dk_ref[rows, lanes] = dk.astype(BF16)
            dv_ref[rows, lanes] = dv.astype(BF16)
            acc[...] = total
            return carry

        lax.fori_loop(0, keys // block, one_block, 0)
        dq_ref[:, lanes] = (acc[...] * HEAD_DIM**-0.5).astype(BF16)
        return carry

    lax.fori_loop(0, 4, one_part, 0)


def add_branch(resid, heads, weight, bias, seg_col, last, result):
    def finish(step, carry):
        rows = rows_at(step)
        branch = dot(heads[rows, :], weight[...]) + bias
        result[rows, :] = resid[rows, :] + jnp.where(seg_col[rows, :] < last, branch, 0.0)
        return carry

    lax.fori_loop(0, resid.shape[0] // CHUNK, finish, 0)


def self_forward_kernel(last, *refs):
    at, hidden, temb, seg_col, seg_row, gain, shift, bias, out_bias, wa, wb, wc, wd = refs[:13]
    resid_zero, queries, key_rows, value_rows, heads, lse, resid_one = refs[13:20]
    wq, wk, wv, wo, lse_rows = refs[20:]
    unpack_weights((wa, wb, wc, wd), (wq, wk, wv), wo)

    def project(step, carry):
        rows = rows_at(step)
        seg = seg_col[rows, :]
        value = hidden[pl.ds(pl.multiple_of(at[0] + step * CHUNK, CHUNK), CHUNK), :].astype(F32)
        added = jnp.zeros_like(value)
        for sentence in range(last + 1):
            added = jnp.where(seg == sentence, temb[sentence : sentence + 1, :], added)
        value = value + added
        resid_zero[rows, :] = value
        normed = (norm_rows(value)[0] * gain[0:1, :] + shift[0:1, :]).astype(BF16)
        query = (dot(normed, wq[...]) + bias[0:1, :]).astype(BF16)
        queries[rows, :] = query * BF16(HEAD_DIM**-0.5)
        key_rows[rows, :] = dot(normed, wk[...]).astype(BF16)
        value_rows[rows, :] = (dot(normed, wv[...]) + bias[1:2, :]).astype(BF16)
        return carry

    lax.fori_loop(0, resid_zero.shape[0] // CHUNK, project, 0)
    attend_rows(queries, key_rows, value_rows, seg_col, seg_row, heads, lse, lse_rows, 128)
    add_branch(resid_zero, heads, wo, out_bias[0:1, :], seg_col, last, resid_one)


def cross_forward_kernel(last, *refs):
    resid_one, memory, seg_col, src_row, gain, shift, bias, out_bias, wa, wb, wc, wd = refs[:12]
    queries, key_rows, value_rows, heads, lse, resid_two = refs[12:18]
    wq, wk, wv, wo, lse_rows = refs[18:]
    unpack_weights((wa, wb, wc, wd), (wq, wk, wv), wo)

    def project(step, carry):
        rows = rows_at(step)
        value = memory[rows, :]
        key_rows[rows, :] = dot(value, wk[...]).astype(BF16)
        value_rows[rows, :] = (dot(value, wv[...]) + bias[3:4, :]).astype(BF16)
        return carry

    lax.fori_loop(0, memory.shape[0] // CHUNK, project, 0)

    def project_queries(step, carry):
        rows = rows_at(step)
        normed = (norm_rows(resid_one[rows, :])[0] * gain[1:2, :] + shift[1:2, :]).astype(BF16)
        query = (dot(normed, wq[...]) + bias[2:3, :]).astype(BF16)
        queries[rows, :] = query * BF16(HEAD_DIM**-0.5)
        return carry

    lax.fori_loop(0, resid_one.shape[0] // CHUNK, project_queries, 0)
    attend_rows(queries, key_rows, value_rows, seg_col, src_row, heads, lse, lse_rows, 128)
    add_branch(resid_one, heads, wo, out_bias[1:2, :], seg_col, last, resid_two)


def ffn_kernel(last, *refs):
    at, resid_two, out_grad, seg_col, gain, shift, bias, out_bias, wa, wb, wc, wd = refs[:12]
    block_out, resid_grad, kept, given, small, bias_grad = refs[12:18]
    normed, normed_t, branch, act, inner_grad, total, normed_grad, weights = refs[18:]
    slots, width = resid_two.shape
    for part, ref in enumerate((wa, wb, wc, wd)):
        weights[part] = ref[...]
    small[...] = jnp.zeros_like(small)
    total[...] = jnp.zeros_like(total)
    normed_grad[...] = jnp.zeros_like(normed_grad)

    def upstream(step):
        place = at[0] + step * CHUNK
        index = place + lax.broadcasted_iota(jnp.int32, (CHUNK, 1), 0)
        below = (index < at[1]).astype(jnp.int32)
        owned = below == 1 - at[2]
        grad = out_grad[pl.ds(pl.multiple_of(place, CHUNK), CHUNK), :].astype(F32)
        return jnp.where(owned, grad, 0.0)

    def prepare(step, carry):
        rows = rows_at(step)
        value = (norm_rows(resid_two[rows, :])[0] * gain[2:3, :] + shift[2:3, :]).astype(BF16)
        normed[rows, :] = value
        real = seg_col[rows, :] < last
        masked = jnp.where(real, upstream(step), 0.0)
        branch[rows, :] = masked.astype(BF16)
        small[2:3, :] += sum_rows(masked)
        return carry

    lax.fori_loop(0, slots // CHUNK, prepare, 0)
    normed_t[...] = jnp.transpose(normed[...])
    block = slots // 2

    def one_pair(pair, carry):
        for half in range(2):
            part = 2 * pair + half
            w_in, w_out = weights.at[part, pl.ds(0, width)], weights.at[part, pl.ds(width, width)]

            def one_block(step, carry):
                rows = rows_at(step, block)
                inner = dot(normed[rows, :], w_in[...]) + bias[pl.ds(part, 1), :]
                below = 0.5 * (1.0 + lax.erf(inner * 0.7071067811865476))
                value = (inner * below).astype(BF16)
                act[rows, :] = value
                slope = below + inner * (0.3989422804014327 * jnp.exp(-0.5 * inner * inner))
                grad = (dot(branch[rows, :], w_out[...], (1, 1)) * slope).astype(BF16)
                inner_grad[rows, :] = grad
                total[rows, :] += dot(value, w_out[...])
                normed_grad[rows, :] += dot(grad, w_in[...], (1, 1))
                return carry

            lax.fori_loop(0, 2, one_block, 0)
            target = (kept, given)[half]
            bias_grad[pl.ds(part, 1), :] = sum_rows(inner_grad[...].astype(F32))
            start = pl.multiple_of(pair * 2 * width, 2 * width)
            target[pl.ds(start, width), :] = dot(normed_t[...], inner_grad[...]).astype(BF16)
            target[pl.ds(start + width, width), :] = dot(act[...], branch[...], (0, 0)).astype(BF16)
        return carry

    lax.fori_loop(0, 2, one_pair, 0)

    def finish(step, carry):
        rows = rows_at(step)
        value = resid_two[rows, :]
        added = jnp.where(seg_col[rows, :] < last, total[rows, :] + out_bias[2:3, :], 0.0)
        block_out[rows, :] = (value + added).astype(BF16)
        xhat, scale = norm_rows(value)
        grad = normed_grad[rows, :]
        small[0:1, :] += sum_rows(grad * xhat)
        small[1:2, :] += sum_rows(grad)
        resid_grad[rows, :] = upstream(step) + norm_back(grad, gain[2:3, :], xhat, scale)
        return carry

    lax.fori_loop(0, slots // CHUNK, finish, 0)


def branch_back(resid_grad, heads, wo, seg_col, last, branch, upper, small, out_grad):
    def one(step, carry):
        rows = rows_at(step)
        masked = jnp.where(seg_col[rows, :] < last, resid_grad[rows, :], 0.0)
        value = masked.astype(BF16)
        branch[rows, :] = value
        small[2:3, :] += sum_rows(value.astype(F32))
        upper[rows, :] = dot(value, wo[...], (1, 1)).astype(BF16)
        return carry

    lax.fori_loop(0, resid_grad.shape[0] // CHUNK, one, 0)
    out_grad[...] = dot(heads[...], branch[...], (0, 0)).astype(BF16)


def cross_backward_kernel(last, *refs):
    resid_grad, resid_one, memory, seg_col, seg_row, src_col, gain, shift = refs[:8]
    queries, key_rows, value_rows, heads, lse, wa, wb, wc, wd = refs[8:17]
    result, memory_grad, kept, given, small = refs[17:22]
    wq, wk, wv, wo, branch, upper, dq, dk, dv, acc, delta, normed = refs[22:34]
    gq, gk, gv, go = refs[34:]
    small[...] = jnp.zeros_like(small)
    unpack_weights((wa, wb, wc, wd), (wq, wk, wv), wo)
    branch_back(resid_grad, heads, wo, seg_col, last, branch, upper, small, go)
    attend_back(
        queries, key_rows, value_rows, upper, heads, lse, seg_row, src_col, dq, dk, dv, acc, delta, 128
    )

    def sources(step, carry):
        rows = rows_at(step)
        value = dv[rows, :]
        small[4:5, :] += sum_rows(value.astype(F32))
        grad = dot(dk[rows, :], wk[...], (1, 1)) + dot(value, wv[...], (1, 1))
        memory_grad[rows, :] = grad.astype(BF16)
        return carry

    lax.fori_loop(0, memory.shape[0] // CHUNK, sources, 0)

    def finish(step, carry):
        rows = rows_at(step)
        xhat, scale = norm_rows(resid_one[rows, :])
        normed[rows, :] = (xhat * gain[1:2, :] + shift[1:2, :]).astype(BF16)
        query_grad = dq[rows, :]
        small[3:4, :] += sum_rows(query_grad.astype(F32))
        grad = dot(query_grad, wq[...], (1, 1))
        small[0:1, :] += sum_rows(grad * xhat)
        small[1:2, :] += sum_rows(grad)
        result[rows, :] = resid_grad[rows, :] + norm_back(grad, gain[1:2, :], xhat, scale)
        return carry

    lax.fori_loop(0, resid_grad.shape[0] // CHUNK, finish, 0)
    gq[...] = dot(normed[...], dq[...], (0, 0)).astype(BF16)
    gk[...] = dot(memory[...], dk[...], (0, 0)).astype(BF16)
    gv[...] = dot(memory[...], dv[...], (0, 0)).astype(BF16)
    store_grads((gq, gk, gv), go, kept, given)


def self_backward_kernel(last, *refs):
    resid_grad, resid_zero, seg_col, seg_row, gain, shift = refs[:6]
    queries, key_rows, value_rows, heads, lse, wa, wb, wc, wd = refs[6:15]
    result, kept, given, small = refs[15:19]
    wq, wk, wv, wo, branch, upper, dq, dk, dv, acc, delta, normed = refs[19:31]
    gq, gk, gv, go = refs[31:]
    small[...] = jnp.zeros_like(small)
    unpack_weights((wa, wb, wc, wd), (wq, wk, wv), wo)
    branch_back(resid_grad, heads, wo, seg_col, last, branch, upper, small, go)
    attend_back(
        queries, key_rows, value_rows, upper, heads, lse, seg_row, seg_col, dq, dk, dv, acc, delta, 128
    )

    def finish(step, carry):
        rows = rows_at(step)
        xhat, scale = norm_rows(resid_zero[rows, :])
        normed[rows, :] = (xhat * gain[0:1, :] + shift[0:1, :]).astype(BF16)
        query_grad, value_grad = dq[rows, :], dv[rows, :]
        small[3:4, :] += sum_rows(query_grad.astype(F32))
        small[4:5, :] += sum_rows(value_grad.astype(F32))
        grad = dot(query_grad, wq[...], (1, 1)) + dot(dk[rows, :], wk[...], (1, 1))
        grad = grad + dot(value_grad, wv[...], (1, 1))
        small[0:1, :] += sum_rows(grad * xhat)
        small[1:2, :] += sum_rows(grad)
        total = resid_grad[rows, :] + norm_back(grad, gain[0:1, :], xhat, scale)
        result[rows, :] = total.astype(BF16)
        return carry

    lax.fori_loop(0, resid_grad.shape[0] // CHUNK, finish, 0)
    gq[...] = dot(normed[...], dq[...], (0, 0)).astype(BF16)
    gk[...] = dot(normed[...], dk[...], (0, 0)).astype(BF16)
    gv[...] = dot(normed[...], dv[...], (0, 0)).astype(BF16)
    store_grads((gq, gk, gv), go, kept, given)


def call(kernel, last, scalars, arrays, outs, scratch, flops):
    name = kernel.__name__.removesuffix("_kernel")
    moved = sum(a.size * a.dtype.itemsize for a in arrays)
    moved += sum(math.prod(s) * jnp.dtype(d).itemsize for s, d in outs)
    return pl.pallas_call(
        partial(kernel, last),
        out_shape=[jax.ShapeDtypeStruct(s, d) for s, d in outs],
        in_specs=[pl.BlockSpec(memory_space=pltpu.SMEM)] * len(scalars)
        + [pl.BlockSpec(memory_space=pltpu.VMEM)] * len(arrays),
        out_specs=[pl.BlockSpec(memory_space=pltpu.VMEM)] * len(outs),
        scratch_shapes=[pltpu.VMEM(s, d) for s, d in scratch],
        compiler_params=pltpu.CompilerParams(vmem_limit_bytes=60 << 20),
        cost_estimate=pl.CostEstimate(flops=flops, bytes_accessed=moved, transcendentals=0),
        name=name,
    )(*scalars, *arrays)


def swap_mp(value):
    return lax.ppermute(value, "mp", [(0, 1), (1, 0)])


def swap_dp(value, bit):
    count = lax.axis_size("dp")
    return lax.ppermute(value, "dp", [(i, i ^ (1 << bit)) for i in range(count)])


def dp_bit(bit):
    return (lax.axis_index("dp") >> bit) & 1


def add_bf16(left, right):
    return (left.astype(jnp.float32) + right.astype(jnp.float32)).astype(jnp.bfloat16)


def reduce_bucket(kept, given):
    total = add_bf16(kept, swap_dp(given, 0))
    rows = total.shape[0] // 2
    total = add_bf16(total[:rows], swap_mp(total[rows:]))
    bits = range(1, lax.axis_size("dp").bit_length() - 1)
    for bit in bits:
        rows = total.shape[0] // 2
        own = dp_bit(bit)
        mine = lax.dynamic_slice_in_dim(total, own * rows, rows, 0)
        other = lax.dynamic_slice_in_dim(total, (1 - own) * rows, rows, 0)
        total = add_bf16(mine, swap_dp(other, bit))
    for bit in reversed(bits):
        other = swap_dp(total, bit)
        high = dp_bit(bit) == 1
        total = jnp.concatenate([jnp.where(high, other, total), jnp.where(high, total, other)])
    return total, swap_dp(total, 0)


def all_sum(value):
    value = value + swap_dp(value, 0)
    value = value + swap_mp(value)
    for bit in range(1, lax.axis_size("dp").bit_length() - 1):
        value = value + swap_dp(value, bit)
    return value


def canonical(parts):
    core, mp = dp_bit(0), lax.axis_index("mp")
    parts = jnp.where(core == 1, parts[jnp.array([1, 0, 3, 2])], parts)
    return jnp.where(mp == 1, parts[jnp.array([2, 3, 0, 1])], parts)


def on_device(
    hidden_in,
    memory,
    tgt_lengths,
    src_lengths,
    timesteps,
    out_grad,
    norm_gain,
    norm_bias,
    self_qkv,
    self_bias,
    self_out,
    cross_q,
    cross_kv,
    cross_bias,
    cross_out,
    ffn_in,
    ffn_in_bias,
    ffn_out,
    out_bias,
):
    row_count, slot_count, model_width = hidden_in.shape
    assert row_count == 1
    segment_count = tgt_lengths.shape[1]
    window = slot_count // 2 + LONGEST // 2
    mp = lax.axis_index("mp")
    local_width = self_qkv.shape[2]
    ends = jnp.cumsum(tgt_lengths[0])
    cut = ends[jnp.argmin(jnp.abs(ends - slot_count // 2))]
    offset = mp * (slot_count - window)
    place = jnp.stack([offset, cut, mp]).astype(jnp.int32)
    tgt_segment = segments_of(tgt_lengths, slot_count)[0]
    tgt_segment = lax.dynamic_slice_in_dim(tgt_segment, offset, window, 0)
    src_segment = segments_of(src_lengths, memory.shape[1])[0]
    seg_col, seg_row = tgt_segment[:, None], tgt_segment[None, :]
    src_col, src_row = src_segment[:, None], src_segment[None, :]
    temb = time_embedding(timesteps[0].astype(jnp.float32), model_width)
    last = segment_count - 1
    width, sources = model_width, memory.shape[1]
    heads_count = 2 * local_width // HEAD_DIM

    def pack_attention(kinds, out):
        cols = [
            [kind[:, 128 * c : 128 * c + 128] for kind in kinds]
            + [out[128 * c : 128 * c + 128, 128 * b : 128 * b + 128] for b in range(width // 128)]
            for c in range(2)
        ]
        return [jnp.concatenate(c) for c in cols]

    def spread(parts):
        core = dp_bit(0)
        first = jnp.where(core == 0, parts[0], parts[1])
        second = jnp.where(core == 0, parts[1], parts[0])
        third = swap_mp(first)
        return first, second, third, swap_dp(third, 0)

    qkv = self_qkv.swapaxes(0, 1)
    kv = cross_kv.swapaxes(0, 1)
    self_w = spread(pack_attention([qkv[0], qkv[1], qkv[2]], self_out))
    small = jnp.concatenate([self_bias, cross_bias, ffn_in_bias.reshape(4, -1)])
    bias_w = jnp.concatenate(spread([small[:4, :128], small[:4, 128:]]), axis=1)
    cross_w = spread(pack_attention([cross_q, kv[0], kv[1]], cross_out))
    hidden_half = ffn_in.shape[1] // 2
    ffn_w = spread(
        [
            jnp.concatenate(
                [
                    ffn_in[:, c * hidden_half : (c + 1) * hidden_half],
                    ffn_out[c * hidden_half : (c + 1) * hidden_half],
                ]
            )
            for c in range(2)
        ]
    )
    ffn_bias = ffn_in_bias.reshape(2, 1, hidden_half)
    ffn_bias = jnp.concatenate(spread([ffn_bias[0], ffn_bias[1]]))

    slots_f32, slots_bf16 = ((window, width), F32), ((window, width), BF16)
    source_bf16, square = ((sources, width), BF16), ((width, width), BF16)
    lse_out = ((heads_count, window), F32)
    attend_scratch = [square] * 4 + [((window, 128), F32)]
    proj = 2 * window * width * width
    self_attend = 4 * window * window * width
    cross_attend = 4 * window * sources * width
    resid_zero, queries, key_rows, value_rows, self_heads, self_lse, resid_one = call(
        self_forward_kernel,
        last,
        [place],
        [hidden_in[0], temb, seg_col, seg_row, norm_gain, norm_bias, bias_w, out_bias, *self_w],
        [slots_f32, slots_bf16, slots_bf16, slots_bf16, slots_bf16, lse_out, slots_f32],
        attend_scratch,
        4 * proj + self_attend,
    )
    cross_queries, cross_keys, cross_values, cross_heads, cross_lse, resid_two = call(
        cross_forward_kernel,
        last,
        [],
        [resid_one, memory[0], seg_col, src_row, norm_gain, norm_bias, bias_w, out_bias, *cross_w],
        [slots_bf16, source_bf16, source_bf16, slots_bf16, lse_out, slots_f32],
        attend_scratch,
        6 * proj + cross_attend,
    )
    ffn_rows = ((4 * width, width), BF16)
    small_out = ((8, width), F32)
    block_out, resid_grad, ffn_kept, ffn_given, small_three, ffn_bias_grad = call(
        ffn_kernel,
        last,
        [place],
        [resid_two, out_grad[0], seg_col, norm_gain, norm_bias, ffn_bias, out_bias, *ffn_w],
        [slots_bf16, slots_f32, ffn_rows, ffn_rows, small_out, ((4, hidden_half), F32)],
        [
            slots_bf16,
            ((width, window), BF16),
            slots_bf16,
            ((window, hidden_half), BF16),
            ((window, hidden_half), BF16),
            slots_f32,
            slots_f32,
            ((4, 2 * width, hidden_half), BF16),
        ],
        24 * proj,
    )

    def tgt_rows(value):
        other = swap_mp(value)
        low, high = jnp.where(mp == 0, value, other), jnp.where(mp == 0, other, value)
        start = slot_count - window
        middle = start + jnp.arange(window - start, dtype=jnp.int32)
        joined = jnp.where((middle < cut)[:, None], low[start:], high[: window - start])
        return jnp.concatenate([low[:start], joined, high[window - start :]])[None]

    block_out = tgt_rows(block_out)
    pack_rows = ((8 * width, 128), BF16)

    def back_scratch(keys):
        return (
            [square] * 4
            + [slots_bf16] * 3
            + [((keys, width), BF16)] * 2
            + [((window, 128), F32), ((heads_count, window), F32), slots_bf16]
            + [square] * 4
        )

    resid_grad, memory_grad, cross_kept, cross_given, small_two = call(
        cross_backward_kernel,
        last,
        [],
        [
            resid_grad,
            resid_one,
            memory[0],
            seg_col,
            seg_row,
            src_col,
            norm_gain,
            norm_bias,
            cross_queries,
            cross_keys,
            cross_values,
            cross_heads,
            cross_lse,
            *cross_w,
        ],
        [slots_f32, source_bf16, pack_rows, pack_rows, small_out],
        back_scratch(sources),
        12 * proj + 5 * cross_attend // 2,
    )
    memory_grad = (
        memory_grad.astype(jnp.float32) + swap_mp(memory_grad).astype(jnp.float32)
    )[None]
    input_grad, self_kept, self_given, small_one = call(
        self_backward_kernel,
        last,
        [],
        [
            resid_grad,
            resid_zero,
            seg_col,
            seg_row,
            norm_gain,
            norm_bias,
            queries,
            key_rows,
            value_rows,
            self_heads,
            self_lse,
            *self_w,
        ],
        [slots_bf16, pack_rows, pack_rows, small_out],
        back_scratch(window),
        8 * proj + 5 * self_attend // 2,
    )
    input_grad = tgt_rows(input_grad).astype(jnp.float32)

    ffn = reduce_bucket(ffn_kept, ffn_given)
    crosses = reduce_bucket(cross_kept, cross_given)
    selves = reduce_bucket(self_kept, self_given)

    def in_order(pair):
        core = dp_bit(0)
        return (
            jnp.where(core == 0, pair[0], pair[1]).astype(F32),
            jnp.where(core == 0, pair[1], pair[0]).astype(F32),
        )

    def attention_grads(pair):
        low, high = in_order(pair)
        kinds = [
            jnp.concatenate([v[k * width : (k + 1) * width] for v in (low, high)], axis=1)
            for k in range(3)
        ]
        out = [
            jnp.concatenate([v[3 * width + 128 * b : 3 * width + 128 * b + 128] for v in (low, high)])
            for b in range(width // 128)
        ]
        return kinds, jnp.concatenate(out, axis=1)

    low, high = in_order(ffn)
    ffn_in_grad = jnp.concatenate([low[:width], high[:width]], axis=1)
    ffn_out_grad = jnp.concatenate([low[width:], high[width:]])
    kinds, cross_out_grad = attention_grads(crosses)
    cross_q_grad, cross_kv_grad = kinds[0], jnp.stack(kinds[1:], axis=1)
    kinds, self_out_grad = attention_grads(selves)
    self_qkv_grad = jnp.stack(kinds, axis=1)

    quarter = width // 4
    split_small = jnp.concatenate([small_one[3:5], small_two[3:5]]).reshape(4, 4, quarter)
    split_small = jnp.concatenate(
        [split_small.swapaxes(0, 1).reshape(4, width), ffn_bias_grad], axis=1
    )
    split_small = canonical(split_small).reshape(8, width)
    small = jnp.concatenate(
        [v[k : k + 1] for k in range(3) for v in (small_one, small_two, small_three)]
        + [split_small]
    )
    small = all_sum(small)
    norm_gain_grad, norm_bias_grad, out_bias_grad = small[:3], small[3:6], small[6:9]
    halves = small[9:].reshape(4, 2, width)
    halves = lax.dynamic_slice_in_dim(halves, mp * 2, 2, 0)
    ffn_in_bias_grad = halves[:, 1].reshape(-1)
    biases = halves[:, 0].reshape(2, 4, quarter).swapaxes(0, 1).reshape(4, 2 * quarter)
    self_bias_grad, cross_bias_grad = biases[:2], biases[2:]
    return (
        block_out,
        input_grad,
        memory_grad,
        norm_gain_grad,
        norm_bias_grad,
        self_qkv_grad,
        self_bias_grad,
        self_out_grad,
        cross_q_grad,
        cross_kv_grad,
        cross_bias_grad,
        cross_out_grad,
        ffn_in_grad,
        ffn_in_bias_grad,
        ffn_out_grad,
        out_bias_grad,
    )


def solution(mesh):
    placed = (
        P("dp", None, None),
        P("dp", None, None),
        P("dp", None),
        P("dp", None),
        P("dp", None),
        P("dp", None, None),
        P(),
        P(),
        P(None, None, "mp"),
        P(None, "mp"),
        P("mp", None),
        P(None, "mp"),
        P(None, None, "mp"),
        P(None, "mp"),
        P("mp", None),
        P(None, "mp"),
        P("mp"),
        P("mp", None),
        P(),
    )
    return jax.shard_map(
        on_device,
        mesh=mesh,
        in_specs=placed,
        out_specs=(
            P("dp", None, None),
            P("dp", None, None),
            P("dp", None, None),
            P(),
            P(),
            P(None, None, "mp"),
            P(None, "mp"),
            P("mp", None),
            P(None, "mp"),
            P(None, None, "mp"),
            P(None, "mp"),
            P("mp", None),
            P(None, "mp"),
            P("mp"),
            P("mp", None),
            P(),
        ),
        check_vma=False,
    )
```
